256 devices in a mesh: ctx: 32 (over z, x), ch: 8 (over y, core).
Axes of the slice: x: 4, y: 4, z: 8, core: 2. Of those that a mesh axis runs over, the one named last changes fastest.
Arguments:
- gate_q: bfloat16 [12288, 4096], P('ctx', 'ch'), may hold values from -6 to 6
- key_k: bfloat16 [12288, 4096], P('ctx', 'ch'), may hold values from -6 to 6
- value_v: bfloat16 [12288, 4096], P('ctx', 'ch'), may hold values from -6 to 6
- long_filter: bfloat16 [12288, 4096], P('ctx', 'ch'), may hold values from -0.0546875 to 0.0546875
- skip_gain: float32 [4096], P('ch'), may hold values from 0.5 to 1.5
- out_weight: bfloat16 [4096, 4096], P('ch'), may hold values from -0.125 to 0.125
Outputs:
- mixed: bfloat16 [12288, 4096], P('ctx', 'ch')
The draws below stay inside these ranges and needn't reach their ends.
All inputs are finite; a program needn't handle non-finite values.
Results may differ from the reference program's by a relative error of at most 0.023.
Values may be sent and summed in bfloat16 or wider, within the bound.
A program may use at most 128 MiB of HBM per device.

```python
import jax
import jax.numpy as jnp
from jax import lax

D = 4096
TOKENS = 12288
N_CH = 8


def spiked(entries, own_key, source, target, parts, factor):
    owner, partner = [(jnp.arange(entries.shape[dim]) // (entries.shape[dim] // parts)).reshape([-1 if axis == dim else 1 for axis in range(entries.ndim)]) for dim in (source, target)]
    chosen = jax.random.permutation(own_key, parts)[partner]
    strong = (owner == chosen) | (owner == (partner + parts // 2) % parts)
    return jnp.where(strong, factor * entries, entries)


def block_levels(rng, shape, shards, low, top_value):
    loudness, own = 1.0, jax.random.fold_in(rng, 6)
    for axis_at, shards_of in shards:
        heights = jnp.exp(jax.random.uniform(jax.random.fold_in(own, axis_at), (shards_of,), jnp.float32, low / len(shards), top_value / len(shards)))
        loudness = loudness * jnp.repeat(heights, shape[axis_at] // shards_of).reshape([-1 if axis == axis_at else 1 for axis in range(len(shape))])
    return loudness


def centred(own_key, extent, deviation, most, shards=(), held_as=jnp.bfloat16):
    drawn = deviation * jax.random.normal(own_key, extent, jnp.float32)
    if shards:
        drawn = drawn * block_levels(own_key, extent, shards, -0.22, 0.18)
    return jnp.clip(drawn, -most, most).astype(held_as)


def gaussian_with(rng, extent, scale, most, split, heavy, dtype=jnp.bfloat16):
    entries = scale * jax.random.normal(rng, extent, jnp.float32)
    if split:
        entries = entries * block_levels(rng, extent, split, -0.22, 0.18)
    return jnp.clip(spiked(entries, jax.random.fold_in(rng, 3), *heavy), -most, most).astype(dtype)


def setup_inputs(seed: int = 0) -> dict:
    key_of = jax.random.split(jax.random.key(seed), 7)
    gate_q = centred(key_of[0], (TOKENS, D), 1.0, 6.0, ((0, 32), (1, 8)))
    key_k = centred(key_of[1], (TOKENS, D), 1.0, 6.0, ((0, 32), (1, 8)))
    value_v = centred(key_of[2], (TOKENS, D), 1.0, 6.0, ((0, 32), (1, 8)))
    long_filter = centred(key_of[3], (TOKENS, D), TOKENS ** -0.5, 0.0546875, ((0, 32), (1, 8)))
    skip_gain = jnp.clip(0.5 + 1.0 * jax.random.uniform(key_of[4], (D,), jnp.float32) ** block_levels(key_of[4], (D,), ((0, 8),), -0.2, 0.2), 0.5, 1.5)
    out_weight = gaussian_with(key_of[5], (D, D), D ** -0.5, 0.125, ((0, 8),), (0, 1, 8, 2.0))
    return dict(gate_q=gate_q, key_k=key_k, value_v=value_v, long_filter=long_filter, skip_gain=skip_gain, out_weight=out_weight)


def reference(gate_q, key_k, value_v, long_filter, skip_gain, out_weight):
    width = D // N_CH
    total = jnp.zeros((TOKENS, D), jnp.float32)
    for group in range(N_CH):
        first = group * width
        gated = (key_k[:, first:first + width].astype(jnp.float32) * value_v[:, first:first + width].astype(jnp.float32)).astype(jnp.bfloat16)
        gated_full = gated.astype(jnp.float32)
        taps = long_filter[:, first:first + width].astype(jnp.float32)
        spectrum = jnp.fft.rfft(gated_full, n=2 * TOKENS, axis=0) * jnp.fft.rfft(taps, n=2 * TOKENS, axis=0)
        conv = jnp.fft.irfft(spectrum, n=2 * TOKENS, axis=0)[:TOKENS].astype(jnp.float32)
        hidden = (gate_q[:, first:first + width].astype(jnp.float32) * (conv + skip_gain[first:first + width][None, :] * gated_full)).astype(jnp.bfloat16)
        partial_value = jnp.dot(hidden, out_weight[first:first + width, :], preferred_element_type=jnp.float32).astype(jnp.bfloat16)
        partial_value = lax.optimization_barrier(partial_value)
        total = total + partial_value.astype(jnp.float32)
    return total.astype(jnp.bfloat16)
```

```python
import jax
import jax.numpy as jnp
import numpy as np
from jax import lax
from jax.sharding import PartitionSpec as P


def tables(blocks, rows):
    half = np.arange(blocks) + 0.5
    outer = 2.0 * np.pi * np.outer(half, np.arange(blocks)) / (2 * blocks)
    twist = 2.0 * np.pi * np.outer(half, np.arange(rows)) / (2 * blocks * rows)
    inner = 2.0 * np.pi * (np.outer(np.arange(rows), np.arange(rows)) % rows) / rows
    return outer, twist, inner


def local(gate_q, key_k, value_v, long_filter, skip_gain, out_weight):
    rows, channels = key_k.shape
    blocks = lax.axis_size("ctx")
    own = channels // blocks
    outer, twist, inner = tables(blocks, rows)
    outer_cos = jnp.asarray(np.cos(outer), jnp.bfloat16)
    outer_sin = jnp.asarray(-np.sin(outer), jnp.bfloat16)
    twist_cos = jnp.asarray(np.cos(twist), jnp.float32)[:, None, :]
    twist_sin = jnp.asarray(np.sin(twist), jnp.float32)[:, None, :]
    cos, sin = np.cos(inner), np.sin(inner)
    ahead = jnp.asarray(np.block([[cos, -sin], [sin, cos]]), jnp.bfloat16)

    gated = (key_k.astype(jnp.float32) * value_v.astype(jnp.float32)).astype(jnp.bfloat16)

    def exchange(value):
        return lax.all_to_all(
            value.reshape(blocks, own, rows), "ctx", split_axis=0, concat_axis=0, tiled=True
        )

    def spectrum(signal):
        re = jnp.einsum("kn,ncp->kcp", outer_cos, signal, preferred_element_type=jnp.float32)
        im = jnp.einsum("kn,ncp->kcp", outer_sin, signal, preferred_element_type=jnp.float32)
        turned = jnp.concatenate(
            [re * twist_cos + im * twist_sin, im * twist_cos - re * twist_sin], axis=2
        ).astype(jnp.bfloat16)
        return jnp.einsum("kcp,pf->kcf", turned, ahead, preferred_element_type=jnp.float32)

    filter_spec = spectrum(exchange(long_filter.T))
    gated_spec = spectrum(exchange(gated.T))
    fr, fi = filter_spec[..., :rows], filter_spec[..., rows:]
    gr, gi = gated_spec[..., :rows], gated_spec[..., rows:]
    product = jnp.concatenate([fr * gr - fi * gi, fr * gi + fi * gr], axis=2).astype(jnp.bfloat16)
    back = jnp.einsum("kcf,pf->kcp", product, ahead, preferred_element_type=jnp.float32)
    br, bi = back[..., :rows], back[..., rows:]
    wound_re = (br * twist_cos - bi * twist_sin).astype(jnp.bfloat16)
    wound_im = (bi * twist_cos + br * twist_sin).astype(jnp.bfloat16)
    finished = jnp.einsum(
        "kn,kcp->ncp", outer_cos, wound_re, preferred_element_type=jnp.float32
    ) + jnp.einsum("kn,kcp->ncp", outer_sin, wound_im, preferred_element_type=jnp.float32)
    finished = (finished * (1.0 / (blocks * rows))).astype(jnp.bfloat16)
    arrived = lax.all_to_all(finished, "ctx", split_axis=0, concat_axis=0, tiled=True)
    conv = arrived.reshape(channels, rows).T.astype(jnp.float32)
    hidden = (
        gate_q.astype(jnp.float32) * (conv + skip_gain[None, :] * gated.astype(jnp.float32))
    ).astype(jnp.bfloat16)
    terms = jnp.dot(hidden, out_weight, preferred_element_type=jnp.float32)
    return lax.psum_scatter(terms.astype(jnp.bfloat16), "ch", scatter_dimension=1, tiled=True)


def solution(mesh):
    placed = (
        P("ctx", "ch"),
        P("ctx", "ch"),
        P("ctx", "ch"),
        P("ctx", "ch"),
        P("ch"),
        P("ch", None),
    )
    return jax.shard_map(
        local, mesh=mesh, in_specs=placed, out_specs=P("ctx", "ch"), check_vma=False
    )
```

```python
import functools

import jax
import jax.numpy as jnp
import numpy as np
from jax import lax
from jax.experimental import pallas as pl
from jax.experimental.pallas import tpu as pltpu
from jax.sharding import PartitionSpec as P

MESH = pl.DeviceIdType.MESH
F32 = jnp.float32
BF16 = jnp.bfloat16
PARTS = 3


def tables(blocks, own, rows):
    half = np.arange(blocks) + 0.5
    outer = 2.0 * np.pi * np.outer(half, np.arange(blocks)) / (2 * blocks)
    twist = 2.0 * np.pi * np.outer(half, np.arange(rows)) / (2 * blocks * rows)
    inner = 2.0 * np.pi * (np.outer(np.arange(rows), np.arange(rows)) % rows) / rows
    wide = np.stack(
        [
            np.repeat(np.cos(outer), own, axis=1),
            np.repeat(-np.sin(outer), own, axis=1),
            np.repeat(np.cos(outer).T, own, axis=1),
            np.repeat(-np.sin(outer).T, own, axis=1),
        ]
    )
    turn = np.stack([np.cos(twist), np.sin(twist)])
    cos, sin = np.cos(inner), np.sin(inner)
    ahead = np.block([[cos, -sin], [sin, cos]])
    return jnp.asarray(wide, F32), jnp.asarray(turn, F32), jnp.asarray(ahead, BF16)


def dot(a, b):
    return jnp.dot(a, b, preferred_element_type=F32)


def far_first(step, count):
    half = (step + 1) // 2
    return (count // 2 + half * (1 - 2 * (step % 2))) % count


def kernel(
    dims,
    q_hbm, k_hbm, v_hbm, f_hbm, skip_ref, w_hbm, wide_ref, turn_ref, ahead_hbm,
    out_ref,
    qb, kb, vb, fb, gated, send_f, send_g, recv_f, recv_g, ahead, kron_f, kron_i, tcos, tsin,
    spec, wound, send_y, recv_y, hid, wx, p_own, p_up, p_down, send_a, recv_a, send_n, recv_n,
    lsem, wl_sem, ws_sem, wr_sem, fs_sem, fr_sem, gs_sem, gr_sem, ys_sem, yr_sem,
    hs_sem, hr_sem, as_sem, ar_sem, ns_sem, nr_sem,
):
    blocks, nx, own, rows, chips = dims
    nz = blocks // nx
    channels = blocks * own
    part = rows // PARTS
    cols = wx.shape[3]
    me = lax.axis_index("ctx")
    mz, mx = me // nx, me % nx
    cj = lax.axis_index("ch")
    y, core = cj // 2, cj % 2
    partner = cj + 1 - 2 * core
    y_up, y_far, y_down = (y + 1) % chips, (y + 2) % chips, (y + 3) % chips
    up, down = y_up * 2 + core, y_down * 2 + core

    def peer(step):
        z = (mz + far_first(step // nx, nz)) % nz
        x = (mx + far_first(step % nx, nx)) % nx
        return z * nx + x

    barrier = pltpu.get_barrier_semaphore()

    def greet(step, carry):
        pl.semaphore_signal(barrier, inc=1, device_id={"ctx": peer(step)}, device_id_type=MESH)
        return carry

    lax.fori_loop(0, blocks - 1, greet, 0)
    for other in (partner, up, down):
        pl.semaphore_signal(barrier, inc=1, device_id={"ch": other}, device_id_type=MESH)

    loads = [
        pltpu.make_async_copy(src, dst, lsem.at[i])
        for i, (src, dst) in enumerate(
            ((f_hbm, fb), (k_hbm, kb), (v_hbm, vb), (ahead_hbm, ahead), (q_hbm, qb))
        )
    ]
    for load in loads:
        load.start()

    def w_cols(yy, cc):
        return w_hbm.at[:, pl.ds(pl.multiple_of((2 * yy + cc) * cols, cols), cols)]

    w_loads = [
        pltpu.make_async_copy(w_cols(yy, core), wx.at[yy, core], wl_sem.at[yy])
        for yy in range(chips)
    ]
    for load in w_loads:
        load.start()

    lane = lax.broadcasted_iota(jnp.int32, (own, channels), 1) % own
    same = lane == lax.broadcasted_iota(jnp.int32, (own, channels), 0)

    def build(i, carry):
        at = pl.ds(pl.multiple_of(i * own, own), own)
        at_im = pl.ds(pl.multiple_of(channels + i * own, own), own)

        def spread(which):
            row = jnp.broadcast_to(wide_ref[which, pl.ds(i, 1), :], (own, channels))
            return jnp.where(same, row, 0.0).astype(BF16)

        kron_f[at, :] = spread(0)
        kron_f[at_im, :] = spread(1)
        kron_i[at, :channels] = spread(2)
        kron_i[at, channels:] = spread(3)
        tcos[at, :] = jnp.broadcast_to(turn_ref[0, pl.ds(i, 1), :], (own, rows))
        tsin[at, :] = jnp.broadcast_to(turn_ref[1, pl.ds(i, 1), :], (own, rows))
        return carry

    lax.fori_loop(0, blocks, build, 0)

    def slab_copy(send, recv, ssem, rsem, target):
        return pltpu.make_async_remote_copy(
            src_ref=send.at[target], dst_ref=recv.at[me],
            send_sem=ssem.at[target], recv_sem=rsem.at[me],
            device_id={"ctx": target}, device_id_type=MESH,
        )

    def send_all(send, recv, ssem, rsem):
        def one(step, carry):
            slab_copy(send, recv, ssem, rsem, peer(step)).start()
            return carry

        lax.fori_loop(0, blocks - 1, one, 0)

    def take_all(send, recv, ssem, rsem):
        def one(step, carry):
            source = (me + step) % blocks
            pltpu.make_async_remote_copy(
                src_ref=send.at[source], dst_ref=recv.at[source],
                send_sem=ssem.at[source], recv_sem=rsem.at[source],
                device_id={"ctx": source}, device_id_type=MESH,
            ).wait_recv()
            return carry

        lax.fori_loop(1, blocks, one, 0)

    def drain(send, recv, ssem, rsem):
        def one(step, carry):
            slab_copy(send, recv, ssem, rsem, peer(step)).wait_send()
            return carry

        lax.fori_loop(0, blocks - 1, one, 0)

    loads[0].wait()
    send_f[...] = fb[...].T.reshape(blocks, own, rows)
    pl.semaphore_wait(barrier, blocks - 1 + 3)
    send_all(send_f, recv_f, fs_sem, fr_sem)
    loads[1].wait()
    loads[2].wait()
    gated[...] = (kb[...].astype(F32) * vb[...].astype(F32)).astype(BF16)
    send_g[...] = gated[...].T.reshape(blocks, own, rows)
    send_all(send_g, recv_g, gs_sem, gr_sem)
    w_sends = [
        pltpu.make_async_remote_copy(
            src_ref=w_cols(yy, 1 - core), dst_ref=wx.at[yy, core],
            send_sem=ws_sem.at[yy], recv_sem=wr_sem.at[yy],
            device_id={"ch": partner}, device_id_type=MESH,
        )
        for yy in range(chips)
    ]
    for copy in w_sends:
        copy.start()
    recv_f[me] = send_f[me]
    recv_g[me] = send_g[me]
    loads[3].wait()
    loads[4].wait()

    def transform(recv):
        both = dot(kron_f[...], recv[...].reshape(channels, rows))
        re, im = both[:channels], both[channels:]
        turned = jnp.concatenate(
            [re * tcos[...] + im * tsin[...], im * tcos[...] - re * tsin[...]], axis=1
        ).astype(BF16)
        return dot(turned, ahead[...])

    take_all(send_f, recv_f, fs_sem, fr_sem)
    spec[...] = transform(recv_f)
    take_all(send_g, recv_g, gs_sem, gr_sem)
    got = transform(recv_g)
    gr, gi = got[:, :rows], got[:, rows:]
    fr, fi = spec[:, :rows], spec[:, rows:]
    product = jnp.concatenate([gr * fr - gi * fi, gr * fi + gi * fr], axis=1).astype(BF16)
    back = lax.dot_general(
        product, ahead[...], (((1,), (1,)), ((), ())), preferred_element_type=F32
    )
    br, bi = back[:, :rows], back[:, rows:]
    wound[:channels, :] = (br * tcos[...] - bi * tsin[...]).astype(BF16)
    wound[channels:, :] = (bi * tcos[...] + br * tsin[...]).astype(BF16)
    for r in range(PARTS):
        done = dot(kron_i[...], wound[:, r * part:(r + 1) * part]) * (1.0 / (blocks * rows))
        send_y[r] = done.astype(BF16).reshape(blocks, own, part)
        send_all(send_y.at[r], recv_y.at[r], ys_sem.at[r], yr_sem.at[r])
        recv_y[r, me] = send_y[r, me]

    for load in w_loads:
        load.wait()
    for copy in w_sends:
        copy.wait()

    half = part // 2

    def towards(r, way, src, dst, ssem, rsem):
        return pltpu.make_async_remote_copy(
            src_ref=src, dst_ref=dst, send_sem=ssem, recv_sem=rsem,
            device_id={"ch": (up, down)[way]}, device_id_type=MESH,
        )

    def far_copy(r, way):
        return towards(r, way, send_a.at[r, way], recv_a.at[r, way], as_sem.at[r, way], ar_sem.at[r, way])

    def near_copy(r, way, h):
        return towards(
            r, way, send_n.at[r, way, h], recv_n.at[r, way, h], ns_sem.at[r, way, h], nr_sem.at[r, way, h]
        )

    def hid_copy(r):
        return pltpu.make_async_remote_copy(
            src_ref=hid.at[core, r], dst_ref=hid.at[core, r],
            send_sem=hs_sem.at[r], recv_sem=hr_sem.at[r],
            device_id={"ch": partner}, device_id_type=MESH,
        )

    def relay(r):
        far_copy(r, 0).wait_recv()
        send_n[r, 0, 0] = (p_up[r] + recv_a[r, 0].astype(F32)).astype(BF16)
        near_copy(r, 0, 0).start()
        far_copy(r, 1).wait_recv()
        send_n[r, 1, 1] = (p_down[r] + recv_a[r, 1].astype(F32)).astype(BF16)
        near_copy(r, 1, 1).start()

    for r in range(PARTS):
        take_all(send_y.at[r], recv_y.at[r], ys_sem.at[r], yr_sem.at[r])
        conv = recv_y[r].reshape(channels, part).astype(F32).T
        at = slice(r * part, (r + 1) * part)
        mixed = conv + skip_ref[...] * gated[at, :].astype(F32)
        hid[core, r] = (qb[at, :].astype(F32) * mixed).astype(BF16)
        hid_copy(r).start()
        hid_copy(r).wait_recv()

        def terms(yy):
            return dot(hid[0, r], wx[yy, 0]) + dot(hid[1, r], wx[yy, 1])

        far = terms(y_far).astype(BF16)
        send_a[r, 0] = far[:half]
        far_copy(r, 0).start()
        send_a[r, 1] = far[half:]
        far_copy(r, 1).start()
        over = terms(y_up)
        send_n[r, 0, 1] = over[half:].astype(BF16)
        near_copy(r, 0, 1).start()
        p_up[r] = over[:half]
        under = terms(y_down)
        send_n[r, 1, 0] = under[:half].astype(BF16)
        near_copy(r, 1, 0).start()
        p_down[r] = under[half:]
        p_own[r] = terms(y)
        if r > 0:
            relay(r - 1)
    relay(PARTS - 1)
    for r in range(PARTS):
        for h in range(2):
            near_copy(r, 0, h).wait_recv()
            near_copy(r, 1, h).wait_recv()
            total = (
                p_own[r, h * half:(h + 1) * half]
                + recv_n[r, 0, h].astype(F32)
                + recv_n[r, 1, h].astype(F32)
            )
            out_ref[r * part + h * half:r * part + (h + 1) * half, :] = total.astype(BF16)

    drain(send_f, recv_f, fs_sem, fr_sem)
    drain(send_g, recv_g, gs_sem, gr_sem)
    for r in range(PARTS):
        drain(send_y.at[r], recv_y.at[r], ys_sem.at[r], yr_sem.at[r])
        hid_copy(r).wait_send()
        for way in range(2):
            far_copy(r, way).wait_send()
            for h in range(2):
                near_copy(r, way, h).wait_send()


def local(sizes, gate_q, key_k, value_v, long_filter, skip_gain, out_weight):
    rows, channels = key_k.shape
    blocks, lines = sizes
    own = channels // blocks
    chips = lines // 2
    cols = out_weight.shape[1] // lines
    nx = 4 if blocks % 4 == 0 else 1
    part = rows // PARTS
    wide, turn, ahead = tables(blocks, own, rows)
    vmem, dma = pltpu.VMEM, pltpu.SemaphoreType.DMA
    whole = pl.BlockSpec(memory_space=pltpu.VMEM)
    away = pl.BlockSpec(memory_space=pl.ANY)
    slabs = vmem((blocks, own, rows), BF16)
    return pl.pallas_call(
        functools.partial(kernel, (blocks, nx, own, rows, chips)),
        out_shape=jax.ShapeDtypeStruct((rows, cols), BF16),
        in_specs=[away, away, away, away, whole, away, whole, whole, away],
        out_specs=whole,
        scratch_shapes=[
            *[vmem((rows, channels), BF16)] * 5,
            slabs, slabs, slabs, slabs,
            vmem((2 * rows, 2 * rows), BF16),
            vmem((2 * channels, channels), BF16),
            vmem((channels, 2 * channels), BF16),
            vmem((channels, rows), F32),
            vmem((channels, rows), F32),
            vmem((channels, 2 * rows), F32),
            vmem((2 * channels, rows), BF16),
            vmem((PARTS, blocks, own, part), BF16),
            vmem((PARTS, blocks, own, part), BF16),
            vmem((2, PARTS, part, channels), BF16),
            vmem((chips, 2, channels, cols), BF16),
            vmem((PARTS, part, cols), F32),
            vmem((PARTS, part // 2, cols), F32),
            vmem((PARTS, part // 2, cols), F32),
            vmem((PARTS, 2, part // 2, cols), BF16),
            vmem((PARTS, 2, part // 2, cols), BF16),
            vmem((PARTS, 2, 2, part // 2, cols), BF16),
            vmem((PARTS, 2, 2, part // 2, cols), BF16),
            dma((5,)), dma((chips,)), dma((chips,)), dma((chips,)),
            dma((blocks,)), dma((blocks,)), dma((blocks,)), dma((blocks,)),
            dma((PARTS, blocks)), dma((PARTS, blocks)),
            dma((PARTS,)), dma((PARTS,)),
            dma((PARTS, 2)), dma((PARTS, 2)),
            dma((PARTS, 2, 2)), dma((PARTS, 2, 2)),
        ],
        compiler_params=pltpu.CompilerParams(
            collective_id=0, has_side_effects=True, vmem_limit_bytes=60 << 20
        ),
    )(gate_q, key_k, value_v, long_filter, skip_gain[None, :], out_weight, wide, turn, ahead)


def solution(mesh):
    placed = (
        P("ctx", "ch"),
        P("ctx", "ch"),
        P("ctx", "ch"),
        P("ctx", "ch"),
        P("ch"),
        P("ch", None),
    )
    sizes = (mesh.shape["ctx"], mesh.shape["ch"])
    return jax.shard_map(
        functools.partial(local, sizes), mesh=mesh, in_specs=placed, out_specs=P("ctx", "ch"),
        check_vma=False,
    )
```

```python
import functools

import jax
import jax.numpy as jnp
import numpy as np
from jax import lax
from jax.experimental import pallas as pl
from jax.experimental.pallas import tpu as pltpu
from jax.sharding import PartitionSpec as P

MESH = pl.DeviceIdType.MESH
F32 = jnp.float32
BF16 = jnp.bfloat16
PARTS = 3


def tables(blocks, own, rows):
    half = np.arange(blocks) + 0.5
    outer = 2.0 * np.pi * np.outer(half, np.arange(blocks)) / (2 * blocks)
    twist = 2.0 * np.pi * np.outer(half, np.arange(rows)) / (2 * blocks * rows)
    inner = 2.0 * np.pi * (np.outer(np.arange(rows), np.arange(rows)) % rows) / rows
    wide = np.stack(
        [
            np.repeat(np.cos(outer), own, axis=1),
            np.repeat(-np.sin(outer), own, axis=1),
            np.repeat(np.cos(outer).T, own, axis=1),
            np.repeat(-np.sin(outer).T, own, axis=1),
        ]
    )
    turn = np.stack([np.cos(twist), np.sin(twist)])
    cos, sin = np.cos(inner), np.sin(inner)
    ahead = np.block([[cos, -sin], [sin, cos]])
    return jnp.asarray(wide, F32), jnp.asarray(turn, F32), jnp.asarray(ahead, BF16)


def dot(a, b):
    return jnp.dot(a, b, preferred_element_type=F32)


def far_first(count):
    return [(count // 2 + (i + 1) // 2 * (1 - 2 * (i % 2))) % count for i in range(count)]


def kernel(
    dims,
    q_hbm, k_hbm, v_hbm, f_hbm, skip_hbm, w_hbm, wide_hbm, turn_hbm, ahead_hbm,
    out_ref,
    skip_ref, wide_ref, turn_ref, qb, kb, vb, fb, gated, send_f, send_g, recv_f, recv_g, ahead, kron_f, kron_i, tcos, tsin,
    spec, wound, send_y, recv_y, hid, wx, first, p_own, p_up, p_down, send_a, recv_a, send_n, recv_n,
    lsem, wl_sem, ws_sem, wr_sem, fs_sem, fr_sem, gs_sem, gr_sem, ys_sem, yr_sem,
    hs_sem, hr_sem, as_sem, ar_sem, ns_sem, nr_sem,
):
    blocks, nx, own, rows, chips = dims
    nz = blocks // nx
    channels = blocks * own
    part = rows // PARTS
    cols = wx.shape[3]
    me = lax.axis_index("ctx")
    mz, mx = me // nx, me % nx
    cj = lax.axis_index("ch")
    y, core = cj // 2, cj % 2
    partner = cj + 1 - 2 * core
    y_up, y_far, y_down = (y + 1) % chips, (y + 2) % chips, (y + 3) % chips
    up, down = y_up * 2 + core, y_down * 2 + core

    zs = [lax.rem(mz + dz, nz) * nx for dz in range(nz)]
    xs = [lax.rem(mx + dx, nx) for dx in range(nx)]
    peers = [zs[dz] + xs[dx] for dz in far_first(nz) for dx in far_first(nx)][:-1]

    barrier = pltpu.get_barrier_semaphore()
    for target in peers:
        pl.semaphore_signal(barrier, inc=1, device_id={"ctx": target}, device_id_type=MESH)
    for other in (partner, up, down):
        pl.semaphore_signal(barrier, inc=1, device_id={"ch": other}, device_id_type=MESH)

    loads = [
        pltpu.make_async_copy(src, dst, lsem.at[i])
        for i, (src, dst) in enumerate(
            (
                (wide_hbm, wide_ref), (turn_hbm, turn_ref), (f_hbm, fb), (k_hbm, kb),
                (v_hbm, vb), (ahead_hbm, ahead), (q_hbm, qb), (skip_hbm, skip_ref),
            )
        )
    ]
    for load in loads:
        load.start()

    def w_cols(yy, cc):
        return w_hbm.at[:, pl.ds(pl.multiple_of((2 * yy + cc) * cols, cols), cols)]

    w_loads = [
        pltpu.make_async_copy(w_cols(yy, core), wx.at[yy, core], wl_sem.at[yy])
        for yy in range(chips)
    ]
    for load in w_loads:
        load.start()

    loads[0].wait()
    loads[1].wait()
    lane = lax.broadcasted_iota(jnp.int32, (own, channels), 1) % own
    same = lane == lax.broadcasted_iota(jnp.int32, (own, channels), 0)

    def build(i, carry):
        at = pl.ds(pl.multiple_of(i * own, own), own)
        at_im = pl.ds(pl.multiple_of(channels + i * own, own), own)

        def spread(which):
            row = jnp.broadcast_to(wide_ref[which, pl.ds(i, 1), :], (own, channels))
            return jnp.where(same, row, 0.0).astype(BF16)

        kron_f[at, :] = spread(0)
        kron_f[at_im, :] = spread(1)
        kron_i[at, :channels] = spread(2)
        kron_i[at, channels:] = spread(3)
        tcos[at, :] = jnp.broadcast_to(turn_ref[0, pl.ds(i, 1), :], (own, rows))
        tsin[at, :] = jnp.broadcast_to(turn_ref[1, pl.ds(i, 1), :], (own, rows))
        return carry

    lax.fori_loop(0, blocks, build, 0)

    def send_all(send, recv, ssem, rsem):
        for target in peers:
            pltpu.make_async_remote_copy(
                src_ref=send.at[target], dst_ref=recv.at[me], send_sem=ssem, recv_sem=rsem,
                device_id={"ctx": target}, device_id_type=MESH,
            ).start()
        pltpu.make_async_copy(send.at[me], recv.at[me], rsem).start()

    def take_all(recv, rsem):
        pltpu.make_async_copy(recv, recv, rsem).wait()

    def drain(send, ssem):
        sent = send.at[pl.ds(0, blocks - 1)]
        pltpu.make_async_copy(sent, sent, ssem).wait()

    loads[2].wait()
    send_f[...] = fb[...].T.reshape(blocks, own, rows)
    pl.semaphore_wait(barrier, blocks - 1 + 3)
    send_all(send_f, recv_f, fs_sem, fr_sem)
    loads[3].wait()
    loads[4].wait()
    gated[...] = (kb[...].astype(F32) * vb[...].astype(F32)).astype(BF16)
    send_g[...] = gated[...].T.reshape(blocks, own, rows)
    send_all(send_g, recv_g, gs_sem, gr_sem)
    w_sends = [
        pltpu.make_async_remote_copy(
            src_ref=w_cols(yy, 1 - core), dst_ref=wx.at[yy, core],
            send_sem=ws_sem.at[yy], recv_sem=wr_sem.at[yy],
            device_id={"ch": partner}, device_id_type=MESH,
        )
        for yy in range(chips)
    ]
    for copy in w_sends:
        copy.start()
    for load in loads[5:]:
        load.wait()

    def transform(recv):
        both = dot(kron_f[...], recv[...].reshape(channels, rows))
        re, im = both[:channels], both[channels:]
        turned = jnp.concatenate(
            [re * tcos[...] + im * tsin[...], im * tcos[...] - re * tsin[...]], axis=1
        ).astype(BF16)
        return dot(turned, ahead[...])

    take_all(recv_f, fr_sem)
    spec[...] = transform(recv_f)
    take_all(recv_g, gr_sem)
    got = transform(recv_g)
    gr, gi = got[:, :rows], got[:, rows:]
    fr, fi = spec[:, :rows], spec[:, rows:]
    product = jnp.concatenate([gr * fr - gi * fi, gr * fi + gi * fr], axis=1).astype(BF16)
    back = lax.dot_general(
        product, ahead[...], (((1,), (1,)), ((), ())), preferred_element_type=F32
    )
    br, bi = back[:, :rows], back[:, rows:]
    wound[:channels, :] = (br * tcos[...] - bi * tsin[...]).astype(BF16)
    wound[channels:, :] = (bi * tcos[...] + br * tsin[...]).astype(BF16)
    for r in range(PARTS):
        done = dot(kron_i[...], wound[:, r * part:(r + 1) * part]) * (1.0 / (blocks * rows))
        send_y[r] = done.astype(BF16).reshape(blocks, own, part)
        send_all(send_y.at[r], recv_y.at[r], ys_sem.at[r], yr_sem.at[r])


    for load in w_loads:
        load.wait()
    for copy in w_sends:
        copy.wait()

    half = part // 2

    def towards(r, way, src, dst, ssem, rsem):
        return pltpu.make_async_remote_copy(
            src_ref=src, dst_ref=dst, send_sem=ssem, recv_sem=rsem,
            device_id={"ch": (up, down)[way]}, device_id_type=MESH,
        )

    def far_copy(r, way):
        return towards(r, way, send_a.at[r, way], recv_a.at[r, way], as_sem.at[r, way], ar_sem.at[r, way])

    def near_copy(r, way, h):
        return towards(
            r, way, send_n.at[r, way, h], recv_n.at[r, way, h], ns_sem.at[r, way, h], nr_sem.at[r, way, h]
        )

    def hid_copy(r):
        return pltpu.make_async_remote_copy(
            src_ref=hid.at[core, r], dst_ref=hid.at[core, r],
            send_sem=hs_sem.at[r], recv_sem=hr_sem.at[r],
            device_id={"ch": partner}, device_id_type=MESH,
        )

    def relay(r):
        far_copy(r, 0).wait_recv()
        send_n[r, 0, 0] = (p_up[r] + recv_a[r, 0].astype(F32)).astype(BF16)
        near_copy(r, 0, 0).start()
        far_copy(r, 1).wait_recv()
        send_n[r, 1, 1] = (p_down[r] + recv_a[r, 1].astype(F32)).astype(BF16)
        near_copy(r, 1, 1).start()

    for r in range(PARTS):
        take_all(recv_y.at[r], yr_sem.at[r])
        conv = recv_y[r].reshape(channels, part).astype(F32).T
        at = slice(r * part, (r + 1) * part)
        mixed = conv + skip_ref[...] * gated[at, :].astype(F32)
        hid[core, r] = (qb[at, :].astype(F32) * mixed).astype(BF16)
        hid_copy(r).start()
        order = (y_far, y_up, y_down, y)
        for i, yy in enumerate(order):
            first[i] = dot(hid[core, r], wx[yy, core])
        hid_copy(r).wait_recv()

        def terms(i):
            return first[i] + dot(hid[1 - core, r], wx[order[i], 1 - core])

        far = terms(0).astype(BF16)
        send_a[r, 0] = far[:half]
        far_copy(r, 0).start()
        send_a[r, 1] = far[half:]
        far_copy(r, 1).start()
        over = terms(1)
        send_n[r, 0, 1] = over[half:].astype(BF16)
        near_copy(r, 0, 1).start()
        p_up[r] = over[:half]
        under = terms(2)
        send_n[r, 1, 0] = under[:half].astype(BF16)
        near_copy(r, 1, 0).start()
        p_down[r] = under[half:]
        p_own[r] = terms(3)
        if r > 0:
            relay(r - 1)
    relay(PARTS - 1)
    for r in range(PARTS):
        for h in range(2):
            near_copy(r, 0, h).wait_recv()
            near_copy(r, 1, h).wait_recv()
            total = (
                p_own[r, h * half:(h + 1) * half]
                + recv_n[r, 0, h].astype(F32)
                + recv_n[r, 1, h].astype(F32)
            )
            out_ref[r * part + h * half:r * part + (h + 1) * half, :] = total

    drain(send_f, fs_sem)
    drain(send_g, gs_sem)
    for r in range(PARTS):
        drain(send_y.at[r], ys_sem.at[r])
        hid_copy(r).wait_send()
        for way in range(2):
            far_copy(r, way).wait_send()
            for h in range(2):
                near_copy(r, way, h).wait_send()


def local(sizes, gate_q, key_k, value_v, long_filter, skip_gain, out_weight):
    rows, channels = key_k.shape
    blocks, lines = sizes
    own = channels // blocks
    chips = lines // 2
    cols = out_weight.shape[1] // lines
    nx = 4 if blocks % 4 == 0 else 1
    part = rows // PARTS
    wide, turn, ahead = tables(blocks, own, rows)
    vmem, dma = pltpu.VMEM, pltpu.SemaphoreType.DMA
    whole = pl.BlockSpec(memory_space=pltpu.VMEM)
    away = pl.BlockSpec(memory_space=pl.ANY)
    slabs = vmem((blocks, own, rows), BF16)
    return pl.pallas_call(
        functools.partial(kernel, (blocks, nx, own, rows, chips)),
        out_shape=jax.ShapeDtypeStruct((rows, cols), F32),
        in_specs=[away] * 9,
        out_specs=whole,
        scratch_shapes=[
            vmem((1, channels), F32), vmem((4, blocks, channels), F32), vmem((2, blocks, rows), F32),
            *[vmem((rows, channels), BF16)] * 5,
            slabs, slabs, slabs, slabs,
            vmem((2 * rows, 2 * rows), BF16),
            vmem((2 * channels, channels), BF16),
            vmem((channels, 2 * channels), BF16),
            vmem((channels, rows), F32),
            vmem((channels, rows), F32),
            vmem((channels, 2 * rows), F32),
            vmem((2 * channels, rows), BF16),
            vmem((PARTS, blocks, own, part), BF16),
            vmem((PARTS, blocks, own, part), BF16),
            vmem((2, PARTS, part, channels), BF16),
            vmem((chips, 2, channels, cols), BF16),
            vmem((4, part, cols), F32),
            vmem((PARTS, part, cols), F32),
            vmem((PARTS, part // 2, cols), F32),
            vmem((PARTS, part // 2, cols), F32),
            vmem((PARTS, 2, part // 2, cols), BF16),
            vmem((PARTS, 2, part // 2, cols), BF16),
            vmem((PARTS, 2, 2, part // 2, cols), BF16),
            vmem((PARTS, 2, 2, part // 2, cols), BF16),
            dma((8,)), dma((chips,)), dma((chips,)), dma((chips,)),
            dma, dma, dma, dma,
            dma((PARTS,)), dma((PARTS,)),
            dma((PARTS,)), dma((PARTS,)),
            dma((PARTS, 2)), dma((PARTS, 2)),
            dma((PARTS, 2, 2)), dma((PARTS, 2, 2)),
        ],
        compiler_params=pltpu.CompilerParams(
            collective_id=0, has_side_effects=True, vmem_limit_bytes=60 << 20
        ),
    )(gate_q, key_k, value_v, long_filter, skip_gain[None, :], out_weight, wide, turn, ahead).astype(BF16)


def solution(mesh):
    placed = (
        P("ctx", "ch"),
        P("ctx", "ch"),
        P("ctx", "ch"),
        P("ctx", "ch"),
        P("ch"),
        P("ch", None),
    )
    sizes = (mesh.shape["ctx"], mesh.shape["ch"])
    return jax.shard_map(
        functools.partial(local, sizes), mesh=mesh, in_specs=placed, out_specs=P("ctx", "ch"),
        check_vma=False,
    )
```

```python
import functools

import jax
import jax.numpy as jnp
import numpy as np
from jax import lax
from jax.experimental import pallas as pl
from jax.experimental.pallas import tpu as pltpu
from jax.sharding import PartitionSpec as P

MESH = pl.DeviceIdType.MESH
F32 = jnp.float32
BF16 = jnp.bfloat16
PARTS = 3


def tables(blocks, own, rows):
    half = np.arange(blocks) + 0.5
    outer = 2.0 * np.pi * np.outer(half, np.arange(blocks)) / (2 * blocks)
    twist = 2.0 * np.pi * np.outer(half, np.arange(rows)) / (2 * blocks * rows)
    inner = 2.0 * np.pi * (np.outer(np.arange(rows), np.arange(rows)) % rows) / rows
    wide = np.stack(
        [
            np.repeat(np.cos(outer), own, axis=1),
            np.repeat(-np.sin(outer), own, axis=1),
            np.repeat(np.cos(outer).T, own, axis=1),
            np.repeat(-np.sin(outer).T, own, axis=1),
        ]
    )
    turn = np.stack([np.cos(twist), np.sin(twist)])
    cos, sin = np.cos(inner), np.sin(inner)
    ahead = np.block([[cos, -sin], [sin, cos]])
    return jnp.asarray(wide, F32), jnp.asarray(turn, F32), jnp.asarray(ahead, BF16)


def dot(a, b):
    return jnp.dot(a, b, preferred_element_type=F32)


def far_first(count):
    return [(count // 2 + (i + 1) // 2 * (1 - 2 * (i % 2))) % count for i in range(count)]


def kernel(
    dims,
    q_hbm, k_hbm, v_hbm, f_hbm, skip_hbm, w_hbm, wide_hbm, turn_hbm, ahead_hbm,
    out_ref,
    skip_ref, wide_ref, turn_ref, qb, kb, vb, fb, gated, send_f, send_g, recv_f, recv_g, ahead, kron_f, kron_i, tcos, tsin,
    spec, wound, send_a_half, recv_a_half, send_y, recv_y, hid, wx, first, p_own, p_up, p_down, send_a, recv_a, send_n, recv_n,
    lsem, wl_sem, ws_sem, wr_sem, fs_sem, fr_sem, gs_sem, gr_sem, as_half, ar_half, ys_sem, yr_sem,
    hs_sem, hr_sem, as_sem, ar_sem, ns_sem, nr_sem,
):
    blocks, nx, own, rows, chips = dims
    few = own // 2
    lot = blocks * few
    nz = blocks // nx
    channels = blocks * own
    part = rows // PARTS
    cols = wx.shape[3]
    me = lax.axis_index("ctx")
    mz, mx = me // nx, me % nx
    cj = lax.axis_index("ch")
    y, core = cj // 2, cj % 2
    partner = cj + 1 - 2 * core
    y_up, y_far, y_down = (y + 1) % chips, (y + 2) % chips, (y + 3) % chips
    up, down = y_up * 2 + core, y_down * 2 + core

    zs = [lax.rem(mz + dz, nz) * nx for dz in range(nz)]
    xs = [lax.rem(mx + dx, nx) for dx in range(nx)]
    peers = [zs[dz] + xs[dx] for dz in far_first(nz) for dx in far_first(nx)][:-1]

    barrier = pltpu.get_barrier_semaphore()
    for target in peers:
        pl.semaphore_signal(barrier, inc=1, device_id={"ctx": target}, device_id_type=MESH)
    for other in (partner, up, down):
        pl.semaphore_signal(barrier, inc=1, device_id={"ch": other}, device_id_type=MESH)

    loads = [
        pltpu.make_async_copy(src, dst, lsem.at[i])
        for i, (src, dst) in enumerate(
            (
                (wide_hbm, wide_ref), (turn_hbm, turn_ref), (f_hbm, fb), (k_hbm, kb),
                (v_hbm, vb), (ahead_hbm, ahead), (q_hbm, qb), (skip_hbm, skip_ref),
            )
        )
    ]
    for load in loads:
        load.start()

    def w_cols(yy, cc):
        return w_hbm.at[:, pl.ds(pl.multiple_of((2 * yy + cc) * cols, cols), cols)]

    w_loads = [
        pltpu.make_async_copy(w_cols(yy, core), wx.at[yy, core], wl_sem.at[yy])
        for yy in range(chips)
    ]
    for load in w_loads:
        load.start()

    loads[0].wait()
    loads[1].wait()
    lane = lax.broadcasted_iota(jnp.int32, (own, lot), 1) % few
    same = lane == lax.broadcasted_iota(jnp.int32, (own, lot), 0) % few

    def build(i, carry):
        at = pl.ds(pl.multiple_of(i * own, own), own)
        at_im = pl.ds(pl.multiple_of(lot + i * own, own), own)

        def pair(table, which, width):
            return jnp.concatenate(
                [jnp.broadcast_to(table[which, pl.ds(2 * i + j, 1), :], (few, width)) for j in range(2)],
                axis=0,
            )

        def spread(which):
            return jnp.where(same, pair(wide_ref, which, lot), 0.0).astype(BF16)

        kron_f[at, :] = spread(0)
        kron_f[at_im, :] = spread(1)
        kron_i[at, :lot] = spread(2)
        kron_i[at, lot:] = spread(3)
        tcos[at, :] = pair(turn_ref, 0, rows)
        tsin[at, :] = pair(turn_ref, 1, rows)
        return carry

    lax.fori_loop(0, blocks // 2, build, 0)

    def send_all(send, recv, ssem, rsem):
        for target in peers:
            pltpu.make_async_remote_copy(
                src_ref=send.at[target], dst_ref=recv.at[me], send_sem=ssem, recv_sem=rsem,
                device_id={"ctx": target}, device_id_type=MESH,
            ).start()
        pltpu.make_async_copy(send.at[me], recv.at[me], rsem).start()

    def take_all(recv, rsem):
        pltpu.make_async_copy(recv, recv, rsem).wait()

    def drain(send, ssem):
        sent = send.at[pl.ds(0, blocks - 1)]
        pltpu.make_async_copy(sent, sent, ssem).wait()

    loads[2].wait()
    send_f[...] = fb[...].astype(F32).T.reshape(blocks, 2, few, rows).astype(BF16)
    pl.semaphore_wait(barrier, blocks - 1 + 3)
    send_all(send_f, recv_f, fs_sem, fr_sem)
    loads[3].wait()
    loads[4].wait()
    rounded = (kb[...].astype(F32) * vb[...].astype(F32)).astype(BF16)
    gated[...] = rounded
    turned_g = rounded.astype(F32).T.reshape(blocks, 2, few, rows)
    for h in range(2):
        send_g[h] = turned_g[:, h].astype(BF16)
        send_all(send_g.at[h], recv_g.at[h], gs_sem.at[h], gr_sem.at[h])
    w_sends = [
        pltpu.make_async_remote_copy(
            src_ref=w_cols(yy, 1 - core), dst_ref=wx.at[yy, core],
            send_sem=ws_sem.at[yy], recv_sem=wr_sem.at[yy],
            device_id={"ch": partner}, device_id_type=MESH,
        )
        for yy in range(chips)
    ]
    for copy in w_sends:
        copy.start()
    for load in loads[5:]:
        load.wait()

    def transform(slabs):
        both = dot(kron_f[...], slabs.astype(F32).reshape(lot, rows).astype(BF16))
        re, im = both[:lot], both[lot:]
        turned = jnp.concatenate(
            [re * tcos[...] + im * tsin[...], im * tcos[...] - re * tsin[...]], axis=1
        ).astype(BF16)
        return dot(turned, ahead[...])

    def convolve(h):
        got = transform(recv_g[h])
        gr, gi = got[:, :rows], got[:, rows:]
        fr, fi = spec[h, :, :rows], spec[h, :, rows:]
        product = jnp.concatenate([gr * fr - gi * fi, gr * fi + gi * fr], axis=1).astype(BF16)
        back = lax.dot_general(
            product, ahead[...], (((1,), (1,)), ((), ())), preferred_element_type=F32
        )
        br, bi = back[:, :rows], back[:, rows:]
        wound[h, :lot, :] = (br * tcos[...] - bi * tsin[...]).astype(BF16)
        wound[h, lot:, :] = (bi * tcos[...] + br * tsin[...]).astype(BF16)

    def finish(h, at, width):
        done = dot(kron_i[...], wound[h, :, at]) * (1.0 / (blocks * rows))
        return done.reshape(blocks, few, width).astype(BF16)

    take_all(recv_f, fr_sem)
    for h in range(2):
        spec[h] = transform(recv_f[:, h])
    take_all(recv_g.at[0], gr_sem.at[0])
    convolve(0)
    send_a_half[...] = finish(0, slice(0, rows), rows)
    send_all(send_a_half, recv_a_half, as_half, ar_half)
    take_all(recv_g.at[1], gr_sem.at[1])
    convolve(1)
    for r in range(PARTS):
        send_y[r] = finish(1, slice(r * part, (r + 1) * part), part)
        send_all(send_y.at[r], recv_y.at[r], ys_sem.at[r], yr_sem.at[r])

    for load in w_loads:
        load.wait()
    for copy in w_sends:
        copy.wait()

    half = part // 2

    def towards(r, way, src, dst, ssem, rsem):
        return pltpu.make_async_remote_copy(
            src_ref=src, dst_ref=dst, send_sem=ssem, recv_sem=rsem,
            device_id={"ch": (up, down)[way]}, device_id_type=MESH,
        )

    def far_copy(r, way):
        return towards(r, way, send_a.at[r, way], recv_a.at[r, way], as_sem.at[r, way], ar_sem.at[r, way])

    def near_copy(r, way, h):
        return towards(
            r, way, send_n.at[r, way, h], recv_n.at[r, way, h], ns_sem.at[r, way, h], nr_sem.at[r, way, h]
        )

    def hid_copy(r):
        return pltpu.make_async_remote_copy(
            src_ref=hid.at[core, r], dst_ref=hid.at[core, r],
            send_sem=hs_sem.at[r], recv_sem=hr_sem.at[r],
            device_id={"ch": partner}, device_id_type=MESH,
        )

    def relay(r):
        far_copy(r, 0).wait_recv()
        send_n[r, 0, 0] = (p_up[r] + recv_a[r, 0].astype(F32)).astype(BF16)
        near_copy(r, 0, 0).start()
        far_copy(r, 1).wait_recv()
        send_n[r, 1, 1] = (p_down[r] + recv_a[r, 1].astype(F32)).astype(BF16)
        near_copy(r, 1, 1).start()

    take_all(recv_a_half, ar_half)
    for r in range(PARTS):
        at = slice(r * part, (r + 1) * part)
        take_all(recv_y.at[r], yr_sem.at[r])
        halves = [recv_a_half[:, :, at].astype(F32), recv_y[r].astype(F32)]
        conv = jnp.stack(halves, axis=1).reshape(channels, part).T
        mixed = conv + skip_ref[...] * gated[at, :].astype(F32)
        hid[core, r] = (qb[at, :].astype(F32) * mixed).astype(BF16)
        hid_copy(r).start()
        order = (y_far, y_up, y_down, y)
        for i, yy in enumerate(order):
            first[i] = dot(hid[core, r], wx[yy, core])
        hid_copy(r).wait_recv()

        def terms(i):
            return first[i] + dot(hid[1 - core, r], wx[order[i], 1 - core])

        far = terms(0).astype(BF16)
        send_a[r, 0] = far[:half]
        far_copy(r, 0).start()
        send_a[r, 1] = far[half:]
        far_copy(r, 1).start()
        over = terms(1)
        send_n[r, 0, 1] = over[half:].astype(BF16)
        near_copy(r, 0, 1).start()
        p_up[r] = over[:half]
        under = terms(2)
        send_n[r, 1, 0] = under[:half].astype(BF16)
        near_copy(r, 1, 0).start()
        p_down[r] = under[half:]
        p_own[r] = terms(3)
        if r > 0:
            relay(r - 1)
    relay(PARTS - 1)
    for r in range(PARTS):
        for h in range(2):
            near_copy(r, 0, h).wait_recv()
            near_copy(r, 1, h).wait_recv()
            total = (
                p_own[r, h * half:(h + 1) * half]
                + recv_n[r, 0, h].astype(F32)
                + recv_n[r, 1, h].astype(F32)
            )
            out_ref[r * part + h * half:r * part + (h + 1) * half, :] = total

    drain(send_f, fs_sem)
    for h in range(2):
        drain(send_g.at[h], gs_sem.at[h])
    drain(send_a_half, as_half)
    for r in range(PARTS):
        drain(send_y.at[r], ys_sem.at[r])
        hid_copy(r).wait_send()
        for way in range(2):
            far_copy(r, way).wait_send()
            for h in range(2):
                near_copy(r, way, h).wait_send()


def local(sizes, gate_q, key_k, value_v, long_filter, skip_gain, out_weight):
    rows, channels = key_k.shape
    blocks, lines = sizes
    own = channels // blocks
    chips = lines // 2
    cols = out_weight.shape[1] // lines
    nx = 4 if blocks % 4 == 0 else 1
    part = rows // PARTS
    few = own // 2
    lot = blocks * few
    wide, turn, ahead = tables(blocks, few, rows)
    vmem, dma = pltpu.VMEM, pltpu.SemaphoreType.DMA
    whole = pl.BlockSpec(memory_space=pltpu.VMEM)
    away = pl.BlockSpec(memory_space=pl.ANY)
    slabs = vmem((blocks, 2, few, rows), BF16)
    split = vmem((2, blocks, few, rows), BF16)
    return pl.pallas_call(
        functools.partial(kernel, (blocks, nx, own, rows, chips)),
        out_shape=pltpu.VMEM((rows, cols), F32),
        in_specs=[away] * 9,
        out_specs=whole,
        scratch_shapes=[
            vmem((1, channels), F32), vmem(wide.shape, F32), vmem((2, blocks, rows), F32),
            *[vmem((rows, channels), BF16)] * 5,
            slabs, split, slabs, split,
            vmem((2 * rows, 2 * rows), BF16),
            vmem((2 * lot, lot), BF16),
            vmem((lot, 2 * lot), BF16),
            vmem((lot, rows), F32),
            vmem((lot, rows), F32),
            vmem((2, lot, 2 * rows), F32),
            vmem((2, 2 * lot, rows), BF16),
            vmem((blocks, few, rows), BF16),
            vmem((blocks, few, rows), BF16),
            vmem((PARTS, blocks, few, part), BF16),
            vmem((PARTS, blocks, few, part), BF16),
            vmem((2, PARTS, part, channels), BF16),
            vmem((chips, 2, channels, cols), BF16),
            vmem((4, part, cols), F32),
            vmem((PARTS, part, cols), F32),
            vmem((PARTS, part // 2, cols), F32),
            vmem((PARTS, part // 2, cols), F32),
            vmem((PARTS, 2, part // 2, cols), BF16),
            vmem((PARTS, 2, part // 2, cols), BF16),
            vmem((PARTS, 2, 2, part // 2, cols), BF16),
            vmem((PARTS, 2, 2, part // 2, cols), BF16),
            dma((8,)), dma((chips,)), dma((chips,)), dma((chips,)),
            dma, dma, dma((2,)), dma((2,)), dma, dma,
            dma((PARTS,)), dma((PARTS,)),
            dma((PARTS,)), dma((PARTS,)),
            dma((PARTS, 2)), dma((PARTS, 2)),
            dma((PARTS, 2, 2)), dma((PARTS, 2, 2)),
        ],
        compiler_params=pltpu.CompilerParams(
            collective_id=0, has_side_effects=True, vmem_limit_bytes=60 << 20
        ),
    )(gate_q, key_k, value_v, long_filter, skip_gain[None, :], out_weight, wide, turn, ahead).astype(BF16)


def solution(mesh):
    placed = (
        P("ctx", "ch"),
        P("ctx", "ch"),
        P("ctx", "ch"),
        P("ctx", "ch"),
        P("ch"),
        P("ch", None),
    )
    sizes = (mesh.shape["ctx"], mesh.shape["ch"])
    return jax.shard_map(
        functools.partial(local, sizes), mesh=mesh, in_specs=placed, out_specs=P("ctx", "ch"),
        check_vma=False,
    )
```

```python
import functools

import jax
import jax.numpy as jnp
import numpy as np
from jax import lax
from jax.experimental import pallas as pl
from jax.experimental.pallas import tpu as pltpu
from jax.sharding import PartitionSpec as P

MESH = pl.DeviceIdType.MESH
F32 = jnp.float32
BF16 = jnp.bfloat16
PARTS = 3


def tables(blocks, own, rows):
    half = np.arange(blocks) + 0.5
    outer = 2.0 * np.pi * np.outer(half, np.arange(blocks)) / (2 * blocks)
    twist = 2.0 * np.pi * np.outer(half, np.arange(rows)) / (2 * blocks * rows)
    inner = 2.0 * np.pi * (np.outer(np.arange(rows), np.arange(rows)) % rows) / rows
    wide = np.stack(
        [
            np.repeat(np.cos(outer), own, axis=1),
            np.repeat(-np.sin(outer), own, axis=1),
            np.repeat(np.cos(outer).T, own, axis=1),
            np.repeat(-np.sin(outer).T, own, axis=1),
        ]
    )
    turn = np.stack([np.cos(twist), np.sin(twist)])
    cos, sin = np.cos(inner), np.sin(inner)
    ahead = np.block([[cos, -sin], [sin, cos]])
    return jnp.asarray(wide, F32), jnp.asarray(turn, F32), jnp.asarray(ahead, BF16)


def dot(a, b):
    return jnp.dot(a, b, preferred_element_type=F32)


def far_first(count):
    return [(count // 2 + (i + 1) // 2 * (1 - 2 * (i % 2))) % count for i in range(count)]


def kernel(
    dims,
    q_hbm, k_hbm, v_hbm, f_hbm, skip_hbm, w_hbm, wide_hbm, turn_hbm, ahead_hbm,
    out_ref,
    skip_ref, wide_ref, turn_ref, qb, kb, vb, fb, gated, send_f, send_g, recv_f, recv_g, ahead, kron_f, kron_i, tcos, tsin,
    spec, wound, send_a_half, recv_a_half, send_a_end, recv_a_end, send_y, recv_y, early, hid, wx, first, p_own, p_up, p_down, send_a, recv_a, send_n, recv_n,
    lsem, wl_sem, ws_sem, wr_sem, fs_sem, fr_sem, gs_sem, gr_sem, as_half, ar_half, as_end, ar_end, ys_sem, yr_sem,
    es_sem, er_sem, hs_sem, hr_sem, as_sem, ar_sem, ns_sem, nr_sem,
):
    blocks, nx, own, rows, chips = dims
    few = own // 2
    lot = blocks * few
    nz = blocks // nx
    channels = blocks * own
    part = rows // PARTS
    cols = wx.shape[3]
    me = lax.axis_index("ctx")
    mz, mx = me // nx, me % nx
    cj = lax.axis_index("ch")
    y, core = cj // 2, cj % 2
    partner = cj + 1 - 2 * core
    y_up, y_far, y_down = (y + 1) % chips, (y + 2) % chips, (y + 3) % chips
    up, down = y_up * 2 + core, y_down * 2 + core

    zs = [lax.rem(mz + dz, nz) * nx for dz in range(nz)]
    xs = [lax.rem(mx + dx, nx) for dx in range(nx)]
    peers = [zs[dz] + xs[dx] for dz in far_first(nz) for dx in far_first(nx)][:-1]

    barrier = pltpu.get_barrier_semaphore()
    for target in peers:
        pl.semaphore_signal(barrier, inc=1, device_id={"ctx": target}, device_id_type=MESH)
    for other in (partner, up, down):
        pl.semaphore_signal(barrier, inc=1, device_id={"ch": other}, device_id_type=MESH)

    loads = [
        pltpu.make_async_copy(src, dst, lsem.at[i])
        for i, (src, dst) in enumerate(
            (
                (wide_hbm, wide_ref), (turn_hbm, turn_ref), (f_hbm, fb), (k_hbm, kb),
                (v_hbm, vb), (ahead_hbm, ahead), (q_hbm, qb), (skip_hbm, skip_ref),
            )
        )
    ]
    for load in loads:
        load.start()

    def w_cols(yy, cc):
        return w_hbm.at[:, pl.ds(pl.multiple_of((2 * yy + cc) * cols, cols), cols)]

    w_loads = [
        pltpu.make_async_copy(w_cols(yy, core), wx.at[yy, core], wl_sem.at[yy])
        for yy in range(chips)
    ]
    for load in w_loads:
        load.start()

    loads[0].wait()
    loads[1].wait()
    lane = lax.broadcasted_iota(jnp.int32, (own, lot), 1) % few
    same = lane == lax.broadcasted_iota(jnp.int32, (own, lot), 0) % few

    def build(i, carry):
        at = pl.ds(pl.multiple_of(i * own, own), own)
        at_im = pl.ds(pl.multiple_of(lot + i * own, own), own)

        def pair(table, which, width):
            return jnp.concatenate(
                [jnp.broadcast_to(table[which, pl.ds(2 * i + j, 1), :], (few, width)) for j in range(2)],
                axis=0,
            )

        def spread(which):
            return jnp.where(same, pair(wide_ref, which, lot), 0.0).astype(BF16)

        kron_f[at, :] = spread(0)
        kron_f[at_im, :] = spread(1)
        kron_i[at, :lot] = spread(2)
        kron_i[at, lot:] = spread(3)
        tcos[at, :] = pair(turn_ref, 0, rows)
        tsin[at, :] = pair(turn_ref, 1, rows)
        return carry

    lax.fori_loop(0, blocks // 2, build, 0)

    def send_all(send, recv, ssem, rsem):
        for target in peers:
            pltpu.make_async_remote_copy(
                src_ref=send.at[target], dst_ref=recv.at[me], send_sem=ssem, recv_sem=rsem,
                device_id={"ctx": target}, device_id_type=MESH,
            ).start()
        pltpu.make_async_copy(send.at[me], recv.at[me], rsem).start()

    def take_all(recv, rsem):
        pltpu.make_async_copy(recv, recv, rsem).wait()

    def drain(send, ssem):
        sent = send.at[pl.ds(0, blocks - 1)]
        pltpu.make_async_copy(sent, sent, ssem).wait()

    loads[2].wait()
    turned_f = fb[...].astype(F32).T.reshape(2, blocks, few, rows)
    for h in range(2):
        send_f[:, h] = turned_f[h].astype(BF16)
    pl.semaphore_wait(barrier, blocks - 1 + 3)
    send_all(send_f, recv_f, fs_sem, fr_sem)
    loads[3].wait()
    loads[4].wait()
    rounded = (kb[...].astype(F32) * vb[...].astype(F32)).astype(BF16)
    gated[...] = rounded
    turned_g = rounded.astype(F32).T.reshape(2, blocks, few, rows)
    for h in range(2):
        send_g[h] = turned_g[h].astype(BF16)
        send_all(send_g.at[h], recv_g.at[h], gs_sem.at[h], gr_sem.at[h])
    w_sends = [
        pltpu.make_async_remote_copy(
            src_ref=w_cols(yy, 1 - core), dst_ref=wx.at[yy, core],
            send_sem=ws_sem.at[yy], recv_sem=wr_sem.at[yy],
            device_id={"ch": partner}, device_id_type=MESH,
        )
        for yy in range(chips)
    ]
    for copy in w_sends:
        copy.start()
    for load in loads[5:]:
        load.wait()

    def transform(slabs):
        both = dot(kron_f[...], slabs.astype(F32).reshape(lot, rows).astype(BF16))
        re, im = both[:lot], both[lot:]
        turned = jnp.concatenate(
            [re * tcos[...] + im * tsin[...], im * tcos[...] - re * tsin[...]], axis=1
        ).astype(BF16)
        return dot(turned, ahead[...])

    def multiply(h):
        got = transform(recv_g[h])
        gr, gi = got[:, :rows], got[:, rows:]
        fr, fi = spec[h, :, :rows], spec[h, :, rows:]
        return jnp.concatenate([gr * fr - gi * fi, gr * fi + gi * fr], axis=1).astype(BF16)

    def finish(product, first_row, last_row):
        at = slice(first_row, last_row)

        def back(kind):
            return lax.dot_general(
                product, ahead[kind * rows + first_row:kind * rows + last_row, :],
                (((1,), (1,)), ((), ())), preferred_element_type=F32,
            )

        br, bi = back(0), back(1)
        wound[:lot, at] = (br * tcos[:, at] - bi * tsin[:, at]).astype(BF16)
        wound[lot:, at] = (bi * tcos[:, at] + br * tsin[:, at]).astype(BF16)
        done = dot(kron_i[...], wound[:, at]) * (1.0 / (blocks * rows))
        return done.reshape(blocks, few, last_row - first_row).astype(BF16)

    last = rows - part
    take_all(recv_f, fr_sem)
    for h in range(2):
        spec[h] = transform(recv_f[:, h])
    take_all(recv_g.at[0], gr_sem.at[0])
    product = multiply(0)
    send_a_half[...] = finish(product, 0, last)
    send_all(send_a_half, recv_a_half, as_half, ar_half)
    send_a_end[...] = finish(product, last, rows)
    take_all(recv_g.at[1], gr_sem.at[1])
    product = multiply(1)
    for r in range(PARTS):
        send_y[r] = finish(product, r * part, (r + 1) * part)
        send_all(send_y.at[r], recv_y.at[r], ys_sem.at[r], yr_sem.at[r])
        if r == 0:
            send_all(send_a_end, recv_a_end, as_end, ar_end)

    for load in w_loads:
        load.wait()
    for copy in w_sends:
        copy.wait()

    half = part // 2

    def towards(r, way, src, dst, ssem, rsem):
        return pltpu.make_async_remote_copy(
            src_ref=src, dst_ref=dst, send_sem=ssem, recv_sem=rsem,
            device_id={"ch": (up, down)[way]}, device_id_type=MESH,
        )

    def far_copy(r, way):
        return towards(r, way, send_a.at[r, way], recv_a.at[r, way], as_sem.at[r, way], ar_sem.at[r, way])

    def near_copy(r, way, h):
        return towards(
            r, way, send_n.at[r, way, h], recv_n.at[r, way, h], ns_sem.at[r, way, h], nr_sem.at[r, way, h]
        )

    def hid_copy(r):
        return pltpu.make_async_remote_copy(
            src_ref=hid.at[core, r], dst_ref=hid.at[core, r],
            send_sem=hs_sem.at[r], recv_sem=hr_sem.at[r],
            device_id={"ch": partner}, device_id_type=MESH,
        )

    spans = (pl.ds(0, last), pl.ds(last, part))

    def early_copy(e):
        view = early.at[core, spans[e]]
        return pltpu.make_async_remote_copy(
            src_ref=view, dst_ref=view, send_sem=es_sem.at[e], recv_sem=er_sem.at[e],
            device_id={"ch": partner}, device_id_type=MESH,
        )

    order = (y_far, y_up, y_down, y)

    def gate(slabs, at, h):
        over = slice(h * lot, (h + 1) * lot)
        conv = slabs.astype(F32).reshape(lot, slabs.shape[2]).T
        mixed = conv + skip_ref[:, over] * gated[at, over].astype(F32)
        return (qb[at, over].astype(F32) * mixed).astype(BF16)

    def relay(r):
        far_copy(r, 0).wait_recv()
        send_n[r, 0, 0] = (p_up[r] + recv_a[r, 0].astype(F32)).astype(BF16)
        near_copy(r, 0, 0).start()
        far_copy(r, 1).wait_recv()
        send_n[r, 1, 1] = (p_down[r] + recv_a[r, 1].astype(F32)).astype(BF16)
        near_copy(r, 1, 1).start()

    def early_begin(e, slabs):
        at = (slice(0, last), slice(last, rows))[e]
        early[core, at] = gate(slabs[...], at, 0)
        early_copy(e).start()
        for i, yy in enumerate(order):
            first[i, at] = dot(early[core, at], wx[yy, core, :lot])

    def early_end(e):
        at = (slice(0, last), slice(last, rows))[e]
        early_copy(e).wait_recv()
        for i, yy in enumerate(order):
            first[i, at] += dot(early[1 - core, at], wx[yy, 1 - core, :lot])

    def begin(r):
        at = slice(r * part, (r + 1) * part)
        take_all(recv_y.at[r], yr_sem.at[r])
        hid[core, r] = gate(recv_y[r], at, 1)
        hid_copy(r).start()
        for i, yy in enumerate(order):
            first[i, at] += dot(hid[core, r], wx[yy, core, lot:])

    def emit(r):
        at = slice(r * part, (r + 1) * part)
        hid_copy(r).wait_recv()

        def terms(i):
            return first[i, at] + dot(hid[1 - core, r], wx[order[i], 1 - core, lot:])

        far = terms(0).astype(BF16)
        send_a[r, 0] = far[:half]
        far_copy(r, 0).start()
        send_a[r, 1] = far[half:]
        far_copy(r, 1).start()
        over = terms(1)
        send_n[r, 0, 1] = over[half:].astype(BF16)
        near_copy(r, 0, 1).start()
        p_up[r] = over[:half]
        under = terms(2)
        send_n[r, 1, 0] = under[:half].astype(BF16)
        near_copy(r, 1, 0).start()
        p_down[r] = under[half:]
        p_own[r] = terms(3)

    take_all(recv_a_half, ar_half)
    early_begin(0, recv_a_half)
    early_end(0)
    begin(0)
    begin(1)
    emit(0)
    take_all(recv_a_end, ar_end)
    early_begin(1, recv_a_end)
    emit(1)
    early_end(1)
    begin(2)
    relay(0)
    emit(2)
    relay(1)
    relay(2)
    for r in range(PARTS):
        for h in range(2):
            near_copy(r, 0, h).wait_recv()
            near_copy(r, 1, h).wait_recv()
            total = (
                p_own[r, h * half:(h + 1) * half]
                + recv_n[r, 0, h].astype(F32)
                + recv_n[r, 1, h].astype(F32)
            )
            out_ref[r * part + h * half:r * part + (h + 1) * half, :] = total

    drain(send_f, fs_sem)
    for h in range(2):
        drain(send_g.at[h], gs_sem.at[h])
    drain(send_a_half, as_half)
    drain(send_a_end, as_end)
    for r in range(PARTS):
        drain(send_y.at[r], ys_sem.at[r])
        hid_copy(r).wait_send()
        if r == 0:
            early_copy(0).wait_send()
            early_copy(1).wait_send()
        for way in range(2):
            far_copy(r, way).wait_send()
            for h in range(2):
                near_copy(r, way, h).wait_send()


def local(sizes, gate_q, key_k, value_v, long_filter, skip_gain, out_weight):
    rows, channels = key_k.shape
    blocks, lines = sizes
    own = channels // blocks
    chips = lines // 2
    cols = out_weight.shape[1] // lines
    nx = 4 if blocks % 4 == 0 else 1
    part = rows // PARTS
    few = own // 2
    lot = blocks * few
    wide, turn, ahead = tables(blocks, few, rows)
    vmem, dma = pltpu.VMEM, pltpu.SemaphoreType.DMA
    whole = pl.BlockSpec(memory_space=pltpu.VMEM)
    away = pl.BlockSpec(memory_space=pl.ANY)
    slabs = vmem((blocks, 2, few, rows), BF16)
    split = vmem((2, blocks, few, rows), BF16)
    return pl.pallas_call(
        functools.partial(kernel, (blocks, nx, own, rows, chips)),
        out_shape=pltpu.VMEM((rows, cols), F32),
        in_specs=[away] * 9,
        out_specs=whole,
        scratch_shapes=[
            vmem((1, channels), F32), vmem(wide.shape, F32), vmem((2, blocks, rows), F32),
            *[vmem((rows, channels), BF16)] * 5,
            slabs, split, slabs, split,
            vmem((2 * rows, 2 * rows), BF16),
            vmem((2 * lot, lot), BF16),
            vmem((lot, 2 * lot), BF16),
            vmem((lot, rows), F32),
            vmem((lot, rows), F32),
            vmem((2, lot, 2 * rows), F32),
            vmem((2 * lot, rows), BF16),
            *[vmem((blocks, few, rows - part), BF16)] * 2,
            *[vmem((blocks, few, part), BF16)] * 2,
            vmem((PARTS, blocks, few, part), BF16),
            vmem((PARTS, blocks, few, part), BF16),
            vmem((2, rows, lot), BF16),
            vmem((2, PARTS, part, lot), BF16),
            vmem((chips, 2, channels, cols), BF16),
            vmem((4, rows, cols), F32),
            vmem((PARTS, part, cols), F32),
            vmem((PARTS, part // 2, cols), F32),
            vmem((PARTS, part // 2, cols), F32),
            vmem((PARTS, 2, part // 2, cols), BF16),
            vmem((PARTS, 2, part // 2, cols), BF16),
            vmem((PARTS, 2, 2, part // 2, cols), BF16),
            vmem((PARTS, 2, 2, part // 2, cols), BF16),
            dma((8,)), dma((chips,)), dma((chips,)), dma((chips,)),
            dma, dma, dma((2,)), dma((2,)), dma, dma, dma, dma,
            dma((PARTS,)), dma((PARTS,)),
            dma((2,)), dma((2,)), dma((PARTS,)), dma((PARTS,)),
            dma((PARTS, 2)), dma((PARTS, 2)),
            dma((PARTS, 2, 2)), dma((PARTS, 2, 2)),
        ],
        compiler_params=pltpu.CompilerParams(
            collective_id=0, has_side_effects=True, vmem_limit_bytes=60 << 20
        ),
    )(gate_q, key_k, value_v, long_filter, skip_gain[None, :], out_weight, wide, turn, ahead).astype(BF16)


def solution(mesh):
    placed = (
        P("ctx", "ch"),
        P("ctx", "ch"),
        P("ctx", "ch"),
        P("ctx", "ch"),
        P("ch"),
        P("ch", None),
    )
    sizes = (mesh.shape["ctx"], mesh.shape["ch"])
    return jax.shard_map(
        functools.partial(local, sizes), mesh=mesh, in_specs=placed, out_specs=P("ctx", "ch"),
        check_vma=False,
    )
```
